32 devices in a mesh: seq: 8 (over y, x, core), head: 4 (over z).
Axes of the slice: x: 2, y: 2, z: 4, core: 2. Of those that a mesh axis runs over, the one named last changes fastest.
Arguments:
- queries: bfloat16 [4096, 16, 128], P('seq', 'head'), may hold values from -4.5 to 4.5
- key_vectors: bfloat16 [4096, 16, 128], P('seq', 'head'), may hold values from -4.5 to 4.5
- value_vectors: bfloat16 [4096, 16, 128], P('seq', 'head'), may hold values from -6 to 6
- feature_map: bfloat16 [128, 256], replicated, may hold values from -0.5 to 0.5
- cotangent: bfloat16 [4096, 16, 128], P('seq', 'head'), may hold values from -6 to 6
Outputs:
- heads_out: bfloat16 [4096, 16, 128], P('seq', 'head')
- grad_query: bfloat16 [4096, 16, 128], P('seq', 'head')
- grad_key: bfloat16 [4096, 16, 128], P('seq', 'head')
- grad_value: bfloat16 [4096, 16, 128], P('seq', 'head')
- grad_feat_map: float32 [128, 256], replicated
The draws below stay inside these ranges and needn't reach their ends.
All inputs are finite; a program needn't handle non-finite values.
Results may differ from the reference program's by a relative error of at most 0.0072.
Values may be sent and summed in bfloat16 or wider, within the bound.
A program may use at most 256 MiB of HBM per device.

```python
import jax
import jax.numpy as jnp
from jax import lax

H = 16
DH = 128
F = 256
WINDOW = 2048
TOK_DEV = 512
TOKENS = 4096
N_SEQ = 8


def query_key_pair(key):
    shape = (TOKENS, H, DH)
    first = jax.random.fold_in(key, 101)
    second = jax.random.fold_in(key, 202)
    query_base = jnp.clip(jax.random.normal(first, shape, jnp.float32), -4.0, 4.0)
    key_base = jnp.clip(jax.random.normal(second, shape, jnp.float32), -4.0, 4.0)
    return (query_base, key_base)


def draw_queries(key, part):
    return query_key_pair(jax.random.fold_in(key, 7))[0].astype(jnp.bfloat16)


def draw_key_vectors(key, part):
    return query_key_pair(jax.random.fold_in(key, 7))[1].astype(jnp.bfloat16)


def shard_levels(rng, shape, cuts, low, top_value):
    gain = 1.0
    for dim, shards_of in cuts:
        steps = jax.random.uniform(jax.random.fold_in(jax.random.fold_in(rng, 6), dim), (shards_of,), jnp.float32, low / len(cuts), top_value / len(cuts))
        gain = gain * jnp.repeat(jnp.exp(steps), shape[dim] // shards_of).reshape((-1,) + (1,) * (len(shape) - 1 - dim))
    return gain


def bell_draw(rng, dims, deviation, reach, cuts=(), kind=jnp.bfloat16):
    entries = jax.random.normal(rng, dims, jnp.float32) * deviation
    if len(cuts) > 0:
        entries = shard_levels(rng, dims, cuts, -0.22, 0.18) * entries
    return jnp.clip(entries, min=-reach, max=reach).astype(kind)


def setup_inputs(seed: int = 0) -> dict:
    arg_keys = jax.random.split(jax.random.key(seed), 6)
    queries = draw_queries(jax.random.fold_in(arg_keys[5], 71), 0)
    key_vectors = draw_key_vectors(jax.random.fold_in(arg_keys[5], 71), 0)
    value_vectors = bell_draw(arg_keys[2], (TOKENS, H, DH), 1.0, 6.0, ((0, 8), (1, 4)))
    feature_map = bell_draw(arg_keys[3], (DH, F), DH ** -0.5, 0.5)
    cotangent = bell_draw(arg_keys[4], (TOKENS, H, DH), 1.0, 6.0, ((0, 8), (1, 4)))
    return {"queries": queries, "key_vectors": key_vectors, "value_vectors": value_vectors, "feature_map": feature_map, "cotangent": cotangent}


highest = lax.Precision.HIGHEST

def widen(array):
    return array.astype(jnp.float32)

def rounded(array):
    return widen(lax.optimization_barrier(array.astype(jnp.bfloat16)))

def feature(values):
    return jnp.where(values > 0, values + 1.0, jnp.exp(values))

def feature_slope(values):
    return jnp.where(values > 0, 1.0, jnp.exp(values))

def reference(queries, key_vectors, value_vectors, feature_map, cotangent):
    scale = DH ** (-0.5)
    query_proj = jnp.einsum('the,ef->thf', widen(queries), widen(feature_map))
    key_proj = jnp.einsum('the,ef->thf', widen(key_vectors), widen(feature_map))
    query_feat = feature(query_proj).astype(jnp.bfloat16)
    key_feat = feature(key_proj).astype(jnp.bfloat16)
    states = jnp.einsum('nshf,nshd->nhfd', widen(key_feat).reshape(N_SEQ, TOK_DEV, H, F), widen(value_vectors).reshape(N_SEQ, TOK_DEV, H, DH))
    prefix_all = jnp.concatenate([jnp.zeros_like(states[:1]), jnp.cumsum(states, axis=0)[:-1]], axis=0)
    pad_keys = jnp.concatenate([jnp.zeros((WINDOW, H, DH), jnp.bfloat16), key_vectors], axis=0)
    pad_values = jnp.concatenate([jnp.zeros((WINDOW, H, DH), jnp.bfloat16), value_vectors], axis=0)
    inner = jnp.arange(TOK_DEV, dtype=jnp.int32)
    lower = inner[:, None] >= inner[None, :]
    extent = jnp.arange(WINDOW + TOK_DEV, dtype=jnp.int32)
    blocks = jnp.arange(N_SEQ, dtype=jnp.int32)

    def window_part(block):
        begin = block * TOK_DEV
        rows_q = lax.dynamic_slice_in_dim(queries, begin, TOK_DEV, 0)
        keys_ext = lax.dynamic_slice_in_dim(pad_keys, begin, WINDOW + TOK_DEV, 0)
        values_ext = lax.dynamic_slice_in_dim(pad_values, begin, WINDOW + TOK_DEV, 0)
        positions = begin + inner
        key_positions = begin - WINDOW + extent
        allowed = (key_positions[None, :] >= 0) & (key_positions[None, :] <= positions[:, None]) & (key_positions[None, :] > positions[:, None] - WINDOW)
        scores = jnp.einsum('thd,shd->hts', widen(rows_q), widen(keys_ext)) * scale
        scores = jnp.where(allowed[None], scores, -jnp.inf)
        peak = lax.optimization_barrier(jnp.max(scores, axis=-1, keepdims=True))
        log_total = peak + jnp.log(lax.optimization_barrier(jnp.sum(jnp.exp(scores - peak), axis=-1, keepdims=True)))
        return (rows_q, keys_ext, values_ext, jnp.exp(scores - log_total))

    def linear_part(block):
        begin = block * TOK_DEV
        feats_q = lax.dynamic_slice_in_dim(query_feat, begin, TOK_DEV, 0)
        feats_k = lax.dynamic_slice_in_dim(key_feat, begin, TOK_DEV, 0)
        values_blk = lax.dynamic_slice_in_dim(value_vectors, begin, TOK_DEV, 0)
        prefix = prefix_all[block]
        affinity = jnp.where(lower[None], jnp.einsum('thf,shf->hts', widen(feats_q), widen(feats_k)), 0.0).astype(jnp.bfloat16)
        numerator = jnp.einsum('hts,shd->thd', widen(affinity), widen(values_blk)) + jnp.einsum('thf,hfd->thd', widen(feats_q), prefix, precision=highest)
        inverse_norm = lax.rsqrt(lax.optimization_barrier(jnp.mean(numerator * numerator, axis=-1, keepdims=True)) + 1e-06)
        return (feats_q, feats_k, values_blk, prefix, affinity, inverse_norm, numerator * inverse_norm)

    def forward_block(block):
        rows_q, keys_ext, values_ext, probs = window_part(block)
        win_out = jnp.einsum('hts,shd->thd', widen(probs.astype(jnp.bfloat16)), widen(values_ext))
        return (win_out + linear_part(block)[6]).astype(jnp.bfloat16)
    heads_out = lax.map(forward_block, blocks).reshape(TOKENS, H, DH)

    def adjoint_block(block):
        begin = block * TOK_DEV
        parts = linear_part(block)
        grads = widen(lax.dynamic_slice_in_dim(cotangent, begin, TOK_DEV, 0))
        lin_out = parts[6]
        grad_numer = (parts[5] * (grads - lin_out * lax.optimization_barrier(jnp.mean(grads * lin_out, axis=-1, keepdims=True)))).astype(jnp.bfloat16)
        adjoint = jnp.einsum('thf,thd->hfd', widen(parts[0]), widen(grad_numer))
        return (grad_numer, adjoint)
    grad_numer_all, adjoints = lax.map(adjoint_block, blocks)
    reverse = jnp.cumsum(adjoints[::-1], axis=0)[::-1]
    suffix_all = jnp.concatenate([reverse[1:], jnp.zeros_like(reverse[:1])], axis=0)

    def backward_step(carry, block):
        key_acc, value_acc = carry
        begin = block * TOK_DEV
        rows_q, keys_ext, values_ext, probs = window_part(block)
        grads = lax.dynamic_slice_in_dim(cotangent, begin, TOK_DEV, 0)
        weight_grad = jnp.einsum('thd,shd->hts', widen(grads), widen(values_ext))
        delta = lax.optimization_barrier(jnp.sum(probs * weight_grad, axis=-1, keepdims=True))
        score_grad = (probs * (weight_grad - delta) * scale).astype(jnp.bfloat16)
        query_win = jnp.einsum('hts,shd->thd', widen(score_grad), widen(keys_ext))
        key_win = rounded(jnp.einsum('hts,thd->shd', widen(score_grad), widen(rows_q)))
        value_win = rounded(jnp.einsum('hts,thd->shd', widen(probs.astype(jnp.bfloat16)), widen(grads)))
        key_acc = lax.dynamic_update_slice_in_dim(key_acc, lax.dynamic_slice_in_dim(key_acc, begin, WINDOW + TOK_DEV, 0) + key_win, begin, 0)
        value_acc = lax.dynamic_update_slice_in_dim(value_acc, lax.dynamic_slice_in_dim(value_acc, begin, WINDOW + TOK_DEV, 0) + value_win, begin, 0)
        feats_q, feats_k, values_blk, prefix, affinity, inverse_norm, lin_out = linear_part(block)
        grad_numer = grad_numer_all[block]
        suffix = suffix_all[block]
        grad_aff = jnp.where(lower[None], jnp.einsum('thd,shd->hts', widen(grad_numer), widen(values_blk)), 0.0).astype(jnp.bfloat16)
        query_feat_grad = jnp.einsum('hts,shf->thf', widen(grad_aff), widen(feats_k)) + jnp.einsum('thd,hfd->thf', widen(grad_numer), prefix, precision=highest)
        key_feat_grad = jnp.einsum('hts,thf->shf', widen(grad_aff), widen(feats_q)) + jnp.einsum('shd,hfd->shf', widen(values_blk), suffix, precision=highest)
        value_lin = jnp.einsum('hts,thd->shd', widen(affinity), widen(grad_numer)) + jnp.einsum('shf,hfd->shd', widen(feats_k), suffix, precision=highest)
        query_slope = (query_feat_grad * feature_slope(lax.dynamic_slice_in_dim(query_proj, begin, TOK_DEV, 0))).astype(jnp.bfloat16)
        key_slope = (key_feat_grad * feature_slope(lax.dynamic_slice_in_dim(key_proj, begin, TOK_DEV, 0))).astype(jnp.bfloat16)
        query_lin = jnp.einsum('thf,ef->the', widen(query_slope), widen(feature_map))
        key_lin = jnp.einsum('thf,ef->the', widen(key_slope), widen(feature_map))
        key_rows = lax.dynamic_slice_in_dim(key_vectors, begin, TOK_DEV, 0)
        map_grad = jnp.einsum('the,thf->ef', widen(rows_q), widen(query_slope)) + jnp.einsum('the,thf->ef', widen(key_rows), widen(key_slope))
        query_total = (query_win + query_lin).astype(jnp.bfloat16)
        return ((key_acc, value_acc), (query_total, key_lin, value_lin, map_grad))
    initial = jnp.zeros((WINDOW + TOKENS, H, DH), jnp.float32)
    (key_acc, value_acc), (query_all, key_lin_all, value_lin_all, map_all) = lax.scan(backward_step, (initial, initial), blocks)
    grad_query = query_all.reshape(TOKENS, H, DH)
    grad_key = (key_acc[WINDOW:] + key_lin_all.reshape(TOKENS, H, DH)).astype(jnp.bfloat16)
    grad_value = (value_acc[WINDOW:] + value_lin_all.reshape(TOKENS, H, DH)).astype(jnp.bfloat16)
    grad_feat_map = lax.optimization_barrier(jnp.sum(map_all, axis=0))
    return (heads_out, grad_query, grad_key, grad_value, grad_feat_map)
```

```python
import functools
import math

import jax
import jax.numpy as jnp
from jax import lax
from jax.experimental import pallas as pl
from jax.experimental.pallas import tpu as pltpu
from jax.sharding import PartitionSpec as P

WINDOW = 2048
LOG2E = math.log2(math.e)
BIG = 1e30
PREFIX_AT = 1
SUFFIX_AT = 3
TURN = 64

f32 = jnp.float32
bf16 = jnp.bfloat16


def nn(a, b):
    return lax.dot_general(a, b, (((1,), (0,)), ((), ())), preferred_element_type=f32)


def nt(a, b):
    return lax.dot_general(a, b, (((1,), (1,)), ((), ())), preferred_element_type=f32)


def tn(a, b):
    return lax.dot_general(a, b, (((0,), (0,)), ((), ())), preferred_element_type=f32)


def split(x):
    high = x.astype(bf16)
    return high, (x - high.astype(f32)).astype(bf16)


def phi(u):
    return jnp.where(u > 0, u + 1.0, jnp.exp(u))


def slope(feat):
    return jnp.minimum(feat, 1.0)


def lower_mask(rows):
    r = lax.broadcasted_iota(jnp.int32, (rows, rows), 0)
    c = lax.broadcasted_iota(jnp.int32, (rows, rows), 1)
    return r >= c


class Copy:
    def __init__(self, src, dst, send, recv, where, sends=None, receives=None):
        self.copy = pltpu.make_async_remote_copy(
            src_ref=src, dst_ref=dst, send_sem=send, recv_sem=recv,
            device_id=where, device_id_type=pl.DeviceIdType.MESH,
        )
        self.sends, self.receives = sends, receives

    def under(self, cond, act):
        if cond is None:
            act()
        else:
            pl.when(cond)(act)

    def start(self):
        self.under(self.sends, lambda: self.copy.start())

    def got(self):
        self.under(self.receives, lambda: self.copy.wait_recv())

    def sent(self):
        self.under(self.sends, lambda: self.copy.wait_send())


def kernel(
    count, lanes,
    query_in, key_in, value_in, fmap_ref, cot_in,
    out_out, gq_out, gk_out, gv_out, gmap_out,
    qd_ref, kv_ref, out_ref, gmap_ref,
    far_ref, r2_ref, third_ref, pr2_ref,
    gfar_ref, gr2_ref, gthird_ref, gpr2_ref, gown_ref, bthird_ref, bpr2_ref, bfar_ref, br2_ref, gd_ref,
    s_ref, e_ref, qphi_ref, kphi_ref, aff_ref, lin_ref, gn_ref, dq_ref, ql_ref, kvl_ref,
    state_ref, other_ref, mine_ref, slots_ref, total_ref, theirs_ref, prefix_ref,
    map_ref, rs_ref, hx_ref, fin_ref,
    kv_send, kv_recv, back_send, back_recv, st_send, st_recv, slot_send, slot_recv,
    rs_send, rs_recv, hx_send, hx_recv, ag_send, ag_recv,
):
    heads, _, rows, width = kv_ref.shape
    device = lax.axis_index("seq")
    lane = lax.axis_index("head")
    core = device % 2
    odd = core == 1
    even = core == 0
    partner = device + 1 - 2 * core
    scale = width ** (-0.5)
    gain = scale * LOG2E
    half = heads // 2
    far_in, far_out = device >= 4, device + 4 < count
    two_in, two_out = device >= 2, device + 2 < count

    def turn(to, get):
        @pl.loop(0, rows // TURN)
        def _(i):
            part = pl.ds(pl.multiple_of(i * TURN, TURN), TURN)
            to(part)[...] = jnp.transpose(get(part), (1, 0, 2))

    def zero_fill():
        @pl.when(jnp.logical_not(far_in))
        def _():
            far_ref[...] = jnp.zeros_like(far_ref)

        @pl.when(jnp.logical_not(far_in) & even)
        def _():
            third_ref[...] = jnp.zeros_like(third_ref)

        @pl.when(jnp.logical_not(two_in))
        def _():
            r2_ref[...] = jnp.zeros_like(r2_ref)
            pr2_ref[...] = jnp.zeros_like(pr2_ref)

        @pl.when(jnp.logical_not(far_in) & odd)
        def _():
            bthird_ref[...] = jnp.zeros_like(bthird_ref)

        @pl.when(jnp.logical_not(two_out))
        def _():
            br2_ref[...] = jnp.zeros_like(br2_ref)

        @pl.when(jnp.logical_not(far_out))
        def _():
            bfar_ref[...] = jnp.zeros_like(bfar_ref)

        for p in range(2):
            for d in range(1, count // 2):
                @pl.when(jnp.logical_not(device + 2 * d < count if p else device >= 2 * d))
                def _():
                    slots_ref[p, d - 1] = jnp.zeros_like(slots_ref[p, d - 1])

        if square:
            @pl.when(one)
            def _():
                br2_ref[pl.ds(0, last)] = jnp.zeros((last,) + br2_ref.shape[1:], bf16)

    square = count == 8
    chip = device // 2
    one, two, three = (chip == 1, chip == 2, chip == 3) if square else (False, False, False)
    last = heads - 1

    barrier = pltpu.get_barrier_semaphore()
    for d in range(1, count):
        pl.semaphore_signal(barrier, inc=1, device_id={"seq": lax.rem(device + d, count)}, device_id_type=pl.DeviceIdType.MESH)
    for d in range(1, lanes):
        pl.semaphore_signal(barrier, inc=1, device_id={"head": lax.rem(lane + d, lanes)}, device_id_type=pl.DeviceIdType.MESH)
    turn(lambda r: kv_ref.at[:, 0, r], lambda r: key_in[r])
    turn(lambda r: kv_ref.at[:, 1, r], lambda r: value_in[r])
    pl.semaphore_wait(barrier, count + lanes - 2)

    def far_copy(h):
        return Copy(kv_ref.at[h], far_ref.at[h], kv_send.at[0, h], kv_recv.at[0, h], {"seq": device + 4}, far_out, far_in)

    def r2_copy(h):
        return Copy(kv_ref.at[h], r2_ref.at[h], kv_send.at[1, h], kv_recv.at[1, h], {"seq": device + 2}, two_out & (chip != 1) if square else two_out, two_in & (chip != 2) if square else two_in)

    def pr2_copy(h):
        return Copy(r2_ref.at[h], pr2_ref.at[h], kv_send.at[2, h], kv_recv.at[2, h], {"seq": partner}, two_in, two_in)

    def own_copy(h):
        return Copy(kv_ref.at[h], third_ref.at[h], kv_send.at[3, h], kv_recv.at[3, h], {"seq": partner}, even, odd)

    def relay_copy(h):
        return Copy(far_ref.at[h], third_ref.at[h], kv_send.at[4, h], kv_recv.at[4, h], {"seq": partner}, odd & far_in, even & far_in)

    def diag_copy(h):
        return Copy(far_ref.at[h], r2_ref.at[h], kv_send.at[5, h], kv_recv.at[5, h], {"seq": device - 2}, three, two)

    def gdiag_copy(h):
        return Copy(gr2_ref.at[h], gd_ref.at[h], back_send.at[4, h], back_recv.at[4, h], {"seq": device + 2}, two & (h < last), three & (h < last))

    def gthird_copy(h):
        return Copy(gthird_ref.at[h], bthird_ref.at[h], back_send.at[0, h], back_recv.at[0, h], {"seq": partner}, odd | far_in, even | far_in)

    def gpr2_copy(h):
        return Copy(gpr2_ref.at[h], bpr2_ref.at[h], back_send.at[1, h], back_recv.at[1, h], {"seq": partner}, two_in, two_in)

    def br2_copy(h):
        return Copy(gr2_ref.at[h], br2_ref.at[h], back_send.at[2, h], back_recv.at[2, h], {"seq": device - 2}, two_in & ((chip != 2) | (h == last)) if square else two_in, two_out & ((chip != 1) | (h == last)) if square else two_out)

    def bfar_copy(h):
        return Copy(gfar_ref.at[h], bfar_ref.at[h], back_send.at[3, h], back_recv.at[3, h], {"seq": device - 4}, far_in, far_out)

    def pair_copy(p):
        return Copy(state_ref.at[p], other_ref.at[p], st_send.at[0, p], st_recv.at[0, p], {"seq": partner})

    def slot_copy(p, d):
        to = device - 2 * d if p else device + 2 * d
        reach, come = device >= 2 * d, device + 2 * d < count
        return Copy(
            mine_ref.at[p], slots_ref.at[p, d - 1], slot_send.at[p, d - 1], slot_recv.at[p, d - 1], {"seq": to},
            reach if p else come, come if p else reach,
        )

    def total_copy(p):
        return Copy(total_ref.at[p], theirs_ref.at[p], st_send.at[1, p], st_recv.at[1, p], {"seq": partner})

    chips = range(1, count // 2)

    def scan_begin(p):
        pair_copy(p).got()
        first = pl.ds(core * half, half)
        mine_ref[p] = (state_ref[p, first] + other_ref[p, first]).astype(bf16)
        for d in chips:
            slot_copy(p, d).start()

    def scan_end(p):
        for d in chips:
            slot_copy(p, d).got()
        total = jnp.zeros(total_ref.shape[1:], f32)
        for d in chips:
            total += slots_ref[p, d - 1].astype(f32)
        total_ref[p] = total
        total_copy(p).start()
        total_copy(p).got()
        use = even if p else odd
        prefix_ref[p, pl.ds(core * half, half)] = total_ref[p]
        prefix_ref[p, pl.ds(half - core * half, half)] = theirs_ref[p]
        prefix_ref[p] += jnp.where(use, other_ref[p], 0.0)

    def outward(h):
        far_copy(h).start()
        r2_copy(h).start()
        own_copy(h).start()

    for h in range(half):
        outward(h)
    turn(lambda r: qd_ref.at[:, 0, r], lambda r: query_in[r])
    turn(lambda r: qd_ref.at[:, 1, r], lambda r: cot_in[r])
    zero_fill()

    @pl.loop(0, heads)
    def _(h):
        feat = phi(nn(kv_ref[h, 0], fmap_ref[...]))
        kphi_ref[h] = feat
        state_ref[0, h] = tn(feat.astype(bf16), kv_ref[h, 1])

    pair_copy(0).start()

    @pl.loop(0, heads)
    def _(h):
        qphi_ref[h] = phi(nn(qd_ref[h, 0], fmap_ref[...]))

    scan_begin(0)
    for h in range(half, heads):
        outward(h)

    @pl.loop(0, heads)
    def _(h):
        affinity = nt(qphi_ref[h].astype(bf16), kphi_ref[h].astype(bf16))
        aff = jnp.where(lower_mask(rows), affinity, 0.0).astype(bf16)
        aff_ref[h] = aff
        lin_ref[h] = nn(aff, kv_ref[h, 1])

    def linear_forward():
        @pl.loop(0, heads)
        def _(h):
            qf = qphi_ref[h].astype(bf16)
            high, low = split(prefix_ref[0, h])
            numer = lin_ref[h] + nn(qf, high) + nn(qf, low)
            inv = lax.rsqrt(jnp.mean(numer * numer, axis=-1, keepdims=True) + 1e-06)
            lin = numer * inv
            grad = qd_ref[h, 1].astype(f32)
            gn = (inv * (grad - lin * jnp.mean(grad * lin, axis=-1, keepdims=True))).astype(bf16)
            lin_ref[h] = lin
            gn_ref[h] = gn
            state_ref[1, h] = tn(qf, gn)

    def add_map(part):
        for i in range(part.shape[1] // width):
            map_ref[pl.ds(i * width, width)] += part[:, i * width : (i + 1) * width]

    def linear_backward_queries():
        map_ref[...] = jnp.zeros_like(map_ref)

        @pl.loop(0, heads)
        def _(h):
            gn = gn_ref[h]
            qphi = qphi_ref[h]
            gaff = jnp.where(lower_mask(rows), nt(gn, kv_ref[h, 1]), 0.0).astype(bf16)
            ph, plo = split(prefix_ref[0, h])
            qfg = nn(gaff, kphi_ref[h].astype(bf16)) + nt(gn, ph) + nt(gn, plo)
            qs = (qfg * slope(qphi)).astype(bf16)
            qphi_ref[h] = tn(gaff, qphi.astype(bf16))
            kvl_ref[h, 1] = tn(aff_ref[h], gn)
            ql_ref[h] = nt(qs, fmap_ref[...])
            add_map(tn(qd_ref[h, 0], qs))

    def linear_backward_keys():
        @pl.loop(0, heads)
        def _(h):
            kphi = kphi_ref[h]
            sh, slo = split(prefix_ref[1, h])
            value = kv_ref[h, 1]
            kfg = qphi_ref[h] + nt(value, sh) + nt(value, slo)
            kf = kphi.astype(bf16)
            kvl_ref[h, 1] += nn(kf, sh) + nn(kf, slo)
            ks = (kfg * slope(kphi)).astype(bf16)
            kvl_ref[h, 0] = nt(ks, fmap_ref[...])
            add_map(tn(kv_ref[h, 0], ks))

    chunk = map_ref.shape[0] // count

    def rs_copy(d):
        to = lax.rem(device + d, count)
        return Copy(map_ref.at[pl.ds(to * chunk, chunk)], rs_ref.at[d - 1], rs_send.at[d - 1], rs_recv.at[d - 1], {"seq": to})

    def hx_copy(d):
        to = lax.rem(lane + d, lanes)
        return Copy(fin_ref.at[0], hx_ref.at[lane], hx_send.at[d - 1], hx_recv.at[d - 1], {"head": to})

    def ag_copy(d):
        to = lax.rem(device + d, count)
        return Copy(fin_ref.at[1], gmap_ref.at[pl.ds(device * chunk, chunk)], ag_send.at[d - 1], ag_recv.at[d - 1], {"seq": to})

    def advance(h):
        far_copy(h).got()
        relay_copy(h).start()
        if square:
            diag_copy(h).start()

    def window(h):
        query = qd_ref[h, 0]
        blocks = (far_ref.at[h], r2_ref.at[h], kv_ref.at[h], pr2_ref.at[h], third_ref.at[h])
        grads = (gfar_ref.at[h], gr2_ref.at[h], gown_ref.at[h], gpr2_ref.at[h], gthird_ref.at[h])
        back = (4, 2, 0, 1 + 2 * core, 3 - 2 * core)
        kj = lax.broadcasted_iota(jnp.int32, (rows, rows), 0)
        qi = lax.broadcasted_iota(jnp.int32, (rows, rows), 1)
        top = None
        for i in (2, 0, 1, 4, 3):
            if i == 1:
                r2_copy(h).got()
                if square:
                    diag_copy(h).got()
                pr2_copy(h).start()
            if i == 4:
                own_copy(h).got()
                relay_copy(h).got()
            if i == 3:
                pr2_copy(h).got()
            s = nt(blocks[i][0], query)
            if i == 0:
                s = jnp.where(kj > qi, s, -BIG)
            if i == 2:
                s = jnp.where(kj <= qi, s, -BIG)
            s_ref[i] = s
            m = jnp.max(s, axis=0, keepdims=True)
            if i != 2:
                m = jnp.where(device >= back[i], m, -BIG)
            top = m if top is None else jnp.maximum(top, m)
        between(h)
        top = top * gain
        total = jnp.zeros((1, rows), f32)
        out = jnp.zeros((width, rows), f32)
        for i in range(5):
            bound = top if i == 2 else jnp.where(device >= back[i], top, BIG)
            e = jnp.exp2(s_ref[i] * gain - bound)
            total += jnp.sum(e, axis=0, keepdims=True)
            eb = e.astype(bf16)
            e_ref[i] = eb
            out += nn(blocks[i][1].T, eb)
        inv = 1.0 / total
        out = out * inv
        grad = qd_ref[h, 1].astype(f32).T
        delta = jnp.sum(grad * out, axis=0, keepdims=True)
        gradn = (grad * inv).astype(bf16)
        gradt = grad.astype(bf16)
        out_ref[h] = out.T
        dq = jnp.zeros((width, rows), f32)
        for i in (4, 3, 0, 1, 2):
            dp = nn(blocks[i][1], gradt)
            eb = e_ref[i]
            ds = (eb.astype(f32) * ((dp - delta) * inv)).astype(bf16)
            grads[i][1] = nt(eb, gradn).astype(bf16)
            grads[i][0] = (nn(ds, query) * scale).astype(bf16)
            dq += nn(blocks[i][0].T, ds)
        dq_ref[h] = (dq * scale).T
        gthird_copy(h).start()
        gpr2_copy(h).start()

    def settle(h):
        gthird_copy(h).got()
        gpr2_copy(h).got()
        gr2_ref[h] = (gr2_ref[h].astype(f32) + jnp.where(two_in, bpr2_ref[h].astype(f32), 0.0)).astype(bf16)
        br2_copy(h).start()
        if square:
            gdiag_copy(h).start()
        t = bthird_ref[h].astype(f32)
        gfar_ref[h] = (gfar_ref[h].astype(f32) + jnp.where(odd, t, 0.0)).astype(bf16)
        if not square:
            bfar_copy(h).start()
        else:
            @pl.when(jnp.logical_not(three) | (h == last))
            def _():
                bfar_copy(h).start()

    def late(h):
        if square:
            @pl.when(three)
            def _():
                gdiag_copy(h).got()
                gfar_ref[h] = (gfar_ref[h].astype(f32) + gd_ref[h].astype(f32)).astype(bf16)
                bfar_copy(h).start()

    def between(h):
        @pl.when(h > 0)
        def _():
            settle(h - 1)

        @pl.when(h > 1)
        def _():
            late(h - 2)

    advance(0)

    @pl.loop(0, heads)
    def _(h):
        @pl.when(h == PREFIX_AT)
        def _():
            scan_end(0)
            linear_forward()
            pair_copy(1).start()
            scan_begin(1)
            linear_backward_queries()

        @pl.when(h == SUFFIX_AT)
        def _():
            scan_end(1)
            linear_backward_keys()
            for d in range(1, count):
                rs_copy(d).start()

        window(h)

        @pl.when(h < last)
        def _():
            advance(h + 1)

    for d in range(1, count):
        rs_copy(d).got()
    part = map_ref[pl.ds(device * chunk, chunk)]
    for d in range(1, count):
        part += rs_ref[d - 1]
    fin_ref[0] = part
    for d in range(1, lanes):
        hx_copy(d).start()
    settle(last)
    late(last - 1)

    turn(lambda r: out_out.at[r], lambda r: (out_ref[:, r] + lin_ref[:, r]).astype(bf16))
    turn(lambda r: gq_out.at[r], lambda r: (dq_ref[:, r] + ql_ref[:, r]).astype(bf16))

    @pl.loop(0, heads)
    def _(h):
        kvl_ref[h] += gown_ref[h].astype(f32) + jnp.where(even, bthird_ref[h].astype(f32), 0.0)

    part = None
    for d in range(1, lanes):
        came = lax.rem(lane + lanes - d, lanes)
        Copy(fin_ref.at[0], hx_ref.at[came], hx_send.at[d - 1], hx_recv.at[d - 1], {"head": lax.rem(lane + d, lanes)}).got()
    hx_ref[lane] = fin_ref[0]
    part = hx_ref[0]
    for d in range(1, lanes):
        part += hx_ref[d]
    fin_ref[1] = part
    for d in range(1, count):
        ag_copy(d).start()
    gmap_ref[pl.ds(device * chunk, chunk)] = part

    @pl.loop(0, heads)
    def _(h):
        br2_copy(h).got()
        bfar_copy(h).got()

    for i, to in enumerate((gk_out, gv_out)):
        turn(lambda r: to.at[r], lambda r: (kvl_ref[:, i, r] + br2_ref[:, i, r].astype(f32) + bfar_ref[:, i, r].astype(f32)).astype(bf16))

    for d in range(1, count):
        came = lax.rem(device + count - d, count)
        Copy(fin_ref.at[1], gmap_ref.at[pl.ds(came * chunk, chunk)], ag_send.at[d - 1], ag_recv.at[d - 1], {"seq": lax.rem(device + d, count)}).got()
    for i in range(gmap_ref.shape[0] // width):
        gmap_out[:, i * width : (i + 1) * width] = gmap_ref[pl.ds(i * width, width)]
    for d in range(1, count):
        rs_copy(d).sent()
        ag_copy(d).sent()
    for d in range(1, lanes):
        hx_copy(d).sent()
    for p in range(2):
        pair_copy(p).sent()
        total_copy(p).sent()
        for d in chips:
            slot_copy(p, d).sent()

    @pl.loop(0, heads)
    def _(h):
        for copy in (far_copy, r2_copy, pr2_copy, own_copy, relay_copy, gthird_copy, gpr2_copy, br2_copy, bfar_copy):
            copy(h).sent()
        if square:
            diag_copy(h).sent()
            gdiag_copy(h).sent()


def on_device(count, lanes, queries, key_vectors, value_vectors, feature_map, cotangent):
    rows, heads, width = queries.shape
    feats = feature_map.shape[1]
    sds = jax.ShapeDtypeStruct
    vmem = pl.BlockSpec(memory_space=pltpu.VMEM)
    V = pltpu.VMEM
    sem = pltpu.SemaphoreType.DMA
    flat = feats
    chunk = flat // count
    two = V((heads, 2, rows, width), bf16)
    wide = V((heads, rows, width), f32)
    state = V((2, heads, feats, width), f32)
    part = V((2, heads // 2, feats, width), f32)
    chips = count // 2 - 1
    low = sds((rows, heads, width), bf16)
    results = pl.pallas_call(
        functools.partial(kernel, count, lanes),
        out_shape=(low, low, low, low, sds((width, feats), f32)),
        in_specs=[vmem] * 5,
        out_specs=(vmem,) * 5,
        scratch_shapes=[two, two, wide, V((flat, width), f32)] + [two] * 14 + [
            V((5, rows, rows), f32), V((5, rows, rows), bf16),
            V((heads, rows, feats), f32), V((heads, rows, feats), f32), V((heads, rows, rows), bf16),
            wide, V((heads, rows, width), bf16), wide, wide, V((heads, 2, rows, width), f32),
            state, state, V((2, heads // 2, feats, width), bf16), V((2, chips, heads // 2, feats, width), bf16), part, part, state,
            V((flat, width), f32), V((count - 1, chunk, width), f32), V((lanes, chunk, width), f32), V((2, chunk, width), f32),
            sem((6, heads)), sem((6, heads)), sem((5, heads)), sem((5, heads)), sem((2, 2)), sem((2, 2)),
            sem((2, chips)), sem((2, chips)), sem((count - 1,)), sem((count - 1,)), sem((lanes - 1,)), sem((lanes - 1,)),
            sem((count - 1,)), sem((count - 1,)),
        ],
        compiler_params=pltpu.CompilerParams(vmem_limit_bytes=60 * 2**20, collective_id=0, has_side_effects=True),
        name="attention",
    )(queries, key_vectors, value_vectors, feature_map, cotangent)
    return hand_over(results)


def hand_over_kernel(*refs):
    number = len(refs) // 3
    came, gives, held, sems = refs[:number], refs[number : 2 * number], refs[2 * number : 3 * number], refs[-1]
    loads = [pltpu.make_async_copy(came[i], held[i], sems.at[0, i]) for i in range(number)]
    stores = [pltpu.make_async_copy(held[i], gives[i], sems.at[1, i]) for i in range(number)]
    for load in loads:
        load.start()
    for load, store in zip(loads, stores):
        load.wait()
        store.start()
    for store in stores:
        store.wait()


def hand_over(results):
    anywhere = pl.BlockSpec(memory_space=pl.ANY)
    return pl.pallas_call(
        hand_over_kernel,
        out_shape=tuple(jax.ShapeDtypeStruct(x.shape, x.dtype) for x in results),
        in_specs=[anywhere] * len(results),
        out_specs=(anywhere,) * len(results),
        scratch_shapes=[pltpu.VMEM(x.shape, x.dtype) for x in results] + [pltpu.SemaphoreType.DMA((2, len(results)))],
        name="hand_over",
    )(*results)


def solution(mesh):
    spread = P("seq", "head", None)
    return jax.shard_map(
        functools.partial(on_device, mesh.shape["seq"], mesh.shape["head"]),
        mesh=mesh,
        in_specs=(spread, spread, spread, P(), spread),
        out_specs=(spread, spread, spread, spread, P()),
        check_vma=False,
    )
```

```python
import functools
import math

import jax
import jax.numpy as jnp
from jax import lax
from jax.experimental import pallas as pl
from jax.experimental.pallas import tpu as pltpu
from jax.sharding import PartitionSpec as P

WINDOW = 2048
LOG2E = math.log2(math.e)
BIG = 1e30
PREFIX_AT = 2
RELAYED = 2
TURN = 64

f32 = jnp.float32
bf16 = jnp.bfloat16


def nn(a, b):
    return lax.dot_general(a, b, (((1,), (0,)), ((), ())), preferred_element_type=f32)


def nt(a, b):
    return lax.dot_general(a, b, (((1,), (1,)), ((), ())), preferred_element_type=f32)


def tn(a, b):
    return lax.dot_general(a, b, (((0,), (0,)), ((), ())), preferred_element_type=f32)


def split(x):
    high = x.astype(bf16)
    return high, (x - high.astype(f32)).astype(bf16)


def phi(u):
    return jnp.where(u > 0, u + 1.0, jnp.exp(u))


def slope(feat):
    return jnp.minimum(feat, 1.0)


def lower_mask(rows):
    r = lax.broadcasted_iota(jnp.int32, (rows, rows), 0)
    c = lax.broadcasted_iota(jnp.int32, (rows, rows), 1)
    return r >= c


class Copy:
    def __init__(self, src, dst, send, recv, where, sends=None, receives=None):
        self.copy = pltpu.make_async_remote_copy(
            src_ref=src, dst_ref=dst, send_sem=send, recv_sem=recv,
            device_id=where, device_id_type=pl.DeviceIdType.MESH,
        )
        self.sends, self.receives = sends, receives

    def under(self, cond, act):
        if cond is None:
            act()
        else:
            pl.when(cond)(act)

    def start(self):
        self.under(self.sends, lambda: self.copy.start())

    def got(self):
        self.under(self.receives, lambda: self.copy.wait_recv())

    def sent(self):
        self.under(self.sends, lambda: self.copy.wait_send())


def kernel(
    count, lanes,
    query_hbm, key_hbm, value_hbm, fmap_ref, cot_hbm,
    out_hbm, gq_hbm, gk_hbm, gv_hbm, gmap_out,
    raw_ref, io_sem, qd_ref, kv_ref, out_ref, gmap_ref,
    far_ref, r2_ref, third_ref, pr2_ref,
    gfar_ref, gr2_ref, gthird_ref, gpr2_ref, gown_ref, bthird_ref, bpr2_ref, bfar_ref, br2_ref, gd_ref,
    s_ref, e_ref, qphi_ref, kphi_ref, aff_ref, lin_ref, gn_ref, dq_ref, kvl_ref,
    state_ref, other_ref, mine_ref, slots_ref, total_ref, theirs_ref, prefix_ref,
    map_ref, rs_ref, hx_ref, fin_ref,
    kv_send, kv_recv, back_send, back_recv, st_send, st_recv, slot_send, slot_recv,
    rs_send, rs_recv, hx_send, hx_recv, ag_send, ag_recv,
):
    heads, _, rows, width = kv_ref.shape
    feats = fmap_ref.shape[1]
    device = lax.axis_index("seq")
    lane = lax.axis_index("head")
    core = device % 2
    odd = core == 1
    even = core == 0
    partner = device + 1 - 2 * core
    scale = width ** (-0.5)
    gain = scale * LOG2E
    half = heads // 2
    far_in, far_out = device >= 4, device + 4 < count
    two_in, two_out = device >= 2, device + 2 < count

    def turn(to, get):
        @pl.loop(0, rows // TURN)
        def _(i):
            part = pl.ds(pl.multiple_of(i * TURN, TURN), TURN)
            to(part)[...] = jnp.transpose(get(part), (1, 0, 2))

    def zero_fill():
        @pl.when(jnp.logical_not(far_in))
        def _():
            far_ref[...] = jnp.zeros_like(far_ref)

        @pl.when(jnp.logical_not(far_in) & even)
        def _():
            third_ref[...] = jnp.zeros_like(third_ref)

        @pl.when(jnp.logical_not(two_in))
        def _():
            r2_ref[...] = jnp.zeros_like(r2_ref)
            pr2_ref[...] = jnp.zeros_like(pr2_ref)

        @pl.when(jnp.logical_not(far_in) & odd)
        def _():
            bthird_ref[...] = jnp.zeros_like(bthird_ref)

        @pl.when(jnp.logical_not(two_out))
        def _():
            br2_ref[...] = jnp.zeros_like(br2_ref)

        @pl.when(jnp.logical_not(far_out))
        def _():
            bfar_ref[...] = jnp.zeros_like(bfar_ref)

        if square:
            @pl.when(chip < 2)
            def _():
                slots_ref[0, 1] = jnp.zeros_like(slots_ref[0, 1])

            @pl.when(chip >= 2)
            def _():
                slots_ref[1, 1] = jnp.zeros_like(slots_ref[1, 1])

            return

        for p in range(2):
            for d in range(1, count // 2):
                @pl.when(jnp.logical_not(device + 2 * d < count if p else device >= 2 * d))
                def _():
                    slots_ref[p, d - 1] = jnp.zeros_like(slots_ref[p, d - 1])

    square = count == 8
    chip = device // 2
    zero, one, two, three = [chip == i if square else False for i in range(4)]
    last = heads - 1

    loads = [
        pltpu.make_async_copy(hbm, raw_ref.at[i], io_sem.at[0, i])
        for i, hbm in enumerate((key_hbm, value_hbm, query_hbm, cot_hbm))
    ]
    stores = [
        pltpu.make_async_copy(raw_ref.at[i], hbm, io_sem.at[1, i])
        for i, hbm in enumerate((out_hbm, gq_hbm, gk_hbm, gv_hbm))
    ]
    for load in loads:
        load.start()
    barrier = pltpu.get_barrier_semaphore()
    for d in range(1, count):
        pl.semaphore_signal(barrier, inc=1, device_id={"seq": lax.rem(device + d, count)}, device_id_type=pl.DeviceIdType.MESH)
    for d in range(1, lanes):
        pl.semaphore_signal(barrier, inc=1, device_id={"head": lax.rem(lane + d, lanes)}, device_id_type=pl.DeviceIdType.MESH)
    for i in range(2):
        loads[i].wait()
        turn(lambda r: kv_ref.at[:, i, r], lambda r: raw_ref[i, r])
    pl.semaphore_wait(barrier, count + lanes - 2)

    def far_copy(h):
        return Copy(kv_ref.at[h], far_ref.at[h], kv_send.at[0, h], kv_recv.at[0, h], {"seq": device + 4}, far_out, far_in)

    def r2_copy(h):
        return Copy(kv_ref.at[h], r2_ref.at[h], kv_send.at[1, h], kv_recv.at[1, h], {"seq": device + 2}, two_out & (chip != 1) if square else two_out, two_in & (chip != 2) if square else two_in)

    def cross_copy(h, i):
        return Copy(kv_ref.at[h, i], r2_ref.at[h, i], kv_send.at[5 + i, h], kv_recv.at[5 + i, h], {"seq": device + 2}, one, two)

    def diag_copy(h, i):
        return Copy(far_ref.at[h, i], r2_ref.at[h, i], kv_send.at[7 + i, h], kv_recv.at[7 + i, h], {"seq": device - 2}, three, two)

    def crosses(h, act):
        if square:
            pl.when(h != 1)(lambda: act(cross_copy(h, 0)))
            pl.when(h == 2)(lambda: act(cross_copy(h, 1)))

    def diagonals(h, act):
        if square:
            pl.when(h == 1)(lambda: act(diag_copy(h, 0)))
            pl.when(h != 2)(lambda: act(diag_copy(h, 1)))

    def pr2_copy(h):
        return Copy(r2_ref.at[h], pr2_ref.at[h], kv_send.at[2, h], kv_recv.at[2, h], {"seq": partner}, two_in, two_in)

    def own_copy(h):
        return Copy(kv_ref.at[h], third_ref.at[h], kv_send.at[3, h], kv_recv.at[3, h], {"seq": partner}, even, odd)

    def relay_copy(h):
        return Copy(far_ref.at[h], third_ref.at[h], kv_send.at[4, h], kv_recv.at[4, h], {"seq": partner}, odd & far_in, even & far_in)

    def gdiag_copy(h):
        return Copy(gr2_ref.at[h], gd_ref.at[h], back_send.at[4, h], back_recv.at[4, h], {"seq": device - 4}, two, zero)

    def gpass_copy(h):
        return Copy(gd_ref.at[h], br2_ref.at[h], back_send.at[5, h], back_recv.at[5, h], {"seq": device + 2}, zero, one)

    def gthird_copy(h):
        return Copy(gthird_ref.at[h], bthird_ref.at[h], back_send.at[0, h], back_recv.at[0, h], {"seq": partner}, odd | far_in, even | far_in)

    def gpr2_copy(h):
        return Copy(gpr2_ref.at[h], bpr2_ref.at[h], back_send.at[1, h], back_recv.at[1, h], {"seq": partner}, two_in, two_in)

    def br2_copy(h):
        return Copy(gr2_ref.at[h], br2_ref.at[h], back_send.at[2, h], back_recv.at[2, h], {"seq": device - 2}, two_in & ((chip != 2) | (h >= RELAYED)) if square else two_in, two_out & ((chip != 1) | (h >= RELAYED)) if square else two_out)

    def bfar_copy(h):
        return Copy(gfar_ref.at[h], bfar_ref.at[h], back_send.at[3, h], back_recv.at[3, h], {"seq": device - 4}, far_in, far_out)

    def pair_copy(p):
        return Copy(state_ref.at[p], other_ref.at[p], st_send.at[0, p], st_recv.at[0, p], {"seq": partner})

    def slot_copy(p, d):
        to = device - 2 * d if p else device + 2 * d
        reach, come = device >= 2 * d, device + 2 * d < count
        return Copy(
            mine_ref.at[p], slots_ref.at[p, d - 1], slot_send.at[p, d - 1], slot_recv.at[p, d - 1], {"seq": to},
            reach if p else come, come if p else reach,
        )

    def total_copy(p):
        return Copy(total_ref.at[p], theirs_ref.at[p], st_send.at[1, p], st_recv.at[1, p], {"seq": partner})

    chips = range(1, count // 2)

    def side_copy(p):
        to = device + 2 - 4 * (chip % 2)
        return Copy(mine_ref.at[p], slots_ref.at[p, 0], slot_send.at[p, 0], slot_recv.at[p, 0], {"seq": to})

    def over_copy(p):
        upper, lower = chip >= 2, chip < 2
        to = device - 4 if p else device + 4
        return Copy(
            slots_ref.at[p, 2], slots_ref.at[p, 1], slot_send.at[p, 1], slot_recv.at[p, 1], {"seq": to},
            upper if p else lower, lower if p else upper,
        )

    def scan_begin(p):
        pair_copy(p).got()
        first = pl.ds(core * half, half)
        mine_ref[p] = (state_ref[p, first] + other_ref[p, first]).astype(bf16)
        if square:
            side_copy(p).start()
        else:
            for d in chips:
                slot_copy(p, d).start()

    def scan_middle(p):
        if square:
            side_copy(p).got()
            slots_ref[p, 2] = (mine_ref[p].astype(f32) + slots_ref[p, 0].astype(f32)).astype(bf16)
            over_copy(p).start()

    def scan_end(p):
        if square:
            over_copy(p).got()
            beside = chip % 2 == (0 if p else 1)
            across = chip < 2 if p else chip >= 2
            total = jnp.where(beside, slots_ref[p, 0].astype(f32), 0.0) + jnp.where(across, slots_ref[p, 1].astype(f32), 0.0)
        else:
            for d in chips:
                slot_copy(p, d).got()
            total = jnp.zeros(total_ref.shape[1:], f32)
            for d in chips:
                total += slots_ref[p, d - 1].astype(f32)
        total_ref[p] = total
        total_copy(p).start()
        total_copy(p).got()
        use = even if p else odd
        prefix_ref[p, pl.ds(core * half, half)] = total_ref[p]
        prefix_ref[p, pl.ds(half - core * half, half)] = theirs_ref[p]
        prefix_ref[p] += jnp.where(use, other_ref[p], 0.0)

    def outward(h):
        far_copy(h).start()
        r2_copy(h).start()
        own_copy(h).start()

    outward(0)
    crosses(0, Copy.start)
    for i in range(2):
        loads[2 + i].wait()
        turn(lambda r: qd_ref.at[:, i, r], lambda r: raw_ref[2 + i, r])

    @pl.loop(0, heads)
    def _(h):
        feat = phi(nn(kv_ref[h, 0], fmap_ref[...]))
        kphi_ref[h] = feat
        state_ref[0, h] = tn(feat.astype(bf16), kv_ref[h, 1])

    pair_copy(0).start()

    @pl.loop(0, heads)
    def _(h):
        qphi_ref[h] = phi(nn(qd_ref[h, 0], fmap_ref[...]))

    zero_fill()
    scan_begin(0)
    outward(1)
    if not square:
        for h in range(2, heads):
            outward(h)

    @pl.loop(0, heads)
    def _(h):
        affinity = nt(qphi_ref[h].astype(bf16), kphi_ref[h].astype(bf16))
        aff = jnp.where(lower_mask(rows), affinity, 0.0).astype(bf16)
        aff_ref[h] = aff
        lin_ref[h] = nn(aff, kv_ref[h, 1])

    def linear_forward():
        @pl.loop(0, heads)
        def _(h):
            qf = qphi_ref[h].astype(bf16)
            high, low = split(prefix_ref[0, h])
            numer = lin_ref[h] + nn(qf, high) + nn(qf, low)
            inv = lax.rsqrt(jnp.mean(numer * numer, axis=-1, keepdims=True) + 1e-06)
            lin = numer * inv
            grad = qd_ref[h, 1].astype(f32)
            gn = (inv * (grad - lin * jnp.mean(grad * lin, axis=-1, keepdims=True))).astype(bf16)
            lin_ref[h] = lin
            gn_ref[h] = gn
            state_ref[1, h] = tn(qf, gn)

    def add_map(part):
        for i in range(part.shape[1] // width):
            map_ref[pl.ds(i * width, width)] += part[:, i * width : (i + 1) * width]

    def linear_backward_queries():
        map_ref[...] = jnp.zeros_like(map_ref)

        @pl.loop(0, heads)
        def _(h):
            gn = gn_ref[h]
            qphi = qphi_ref[h]
            gaff = jnp.where(lower_mask(rows), nt(gn, kv_ref[h, 1]), 0.0).astype(bf16)
            ph, plo = split(prefix_ref[0, h])
            qfg = nn(gaff, kphi_ref[h].astype(bf16)) + nt(gn, ph) + nt(gn, plo)
            qs = (qfg * slope(qphi)).astype(bf16)
            qphi_ref[h] = tn(gaff, qphi.astype(bf16))
            kvl_ref[h, 1] = tn(aff_ref[h], gn)
            aff_ref[h, :, pl.ds(0, feats)] = qs
            add_map(tn(qd_ref[h, 0], qs))

    def linear_backward_keys():
        @pl.loop(0, heads)
        def _(h):
            kphi = kphi_ref[h]
            sh, slo = split(prefix_ref[1, h])
            value = kv_ref[h, 1]
            kfg = qphi_ref[h] + nt(value, sh) + nt(value, slo)
            ks = (kfg * slope(kphi)).astype(bf16)
            aff_ref[h, :, pl.ds(rows - feats, feats)] = ks
            add_map(tn(kv_ref[h, 0], ks))

    def linear_outputs():
        @pl.loop(0, heads)
        def _(h):
            sh, slo = split(prefix_ref[1, h])
            kf = kphi_ref[h].astype(bf16)
            dq_ref[h] += nt(aff_ref[h, :, pl.ds(0, feats)], fmap_ref[...])
            kvl_ref[h, 0] = nt(aff_ref[h, :, pl.ds(rows - feats, feats)], fmap_ref[...])
            kvl_ref[h, 1] += nn(kf, sh) + nn(kf, slo)

    chunk = map_ref.shape[0] // count

    def rs_copy(d):
        to = lax.rem(device + d, count)
        return Copy(map_ref.at[pl.ds(to * chunk, chunk)], rs_ref.at[d - 1], rs_send.at[d - 1], rs_recv.at[d - 1], {"seq": to})

    def hx_copy(d):
        to = lax.rem(lane + d, lanes)
        return Copy(fin_ref.at[0], hx_ref.at[lane], hx_send.at[d - 1], hx_recv.at[d - 1], {"head": to})

    def ag_copy(d):
        to = lax.rem(device + d, count)
        return Copy(fin_ref.at[1], gmap_ref.at[pl.ds(device * chunk, chunk)], ag_send.at[d - 1], ag_recv.at[d - 1], {"seq": to})

    def relayed(h, act):
        pl.when(h < RELAYED)(act)

    def advance(h):
        far_copy(h).got()
        relay_copy(h).start()
        diagonals(h, Copy.start)

    def window(h):
        query = qd_ref[h, 0]
        blocks = (far_ref.at[h], r2_ref.at[h], kv_ref.at[h], pr2_ref.at[h], third_ref.at[h])
        grads = (gfar_ref.at[h], gr2_ref.at[h], gown_ref.at[h], gpr2_ref.at[h], gthird_ref.at[h])
        back = (4, 2, 0, 1 + 2 * core, 3 - 2 * core)
        kj = lax.broadcasted_iota(jnp.int32, (rows, rows), 0)
        qi = lax.broadcasted_iota(jnp.int32, (rows, rows), 1)
        top = None
        r2_copy(h).got()
        crosses(h, Copy.got)
        diagonals(h, Copy.got)
        pr2_copy(h).start()
        for i in (2, 0, 1, 4, 3):
            if i == 4:
                own_copy(h).got()
                relay_copy(h).got()
            if i == 3:
                pr2_copy(h).got()
            s = nt(blocks[i][0], query)
            if i == 0:
                s = jnp.where(kj > qi, s, -BIG)
            if i == 2:
                s = jnp.where(kj <= qi, s, -BIG)
            s_ref[i] = s
            m = jnp.max(s, axis=0, keepdims=True)
            if i != 2:
                m = jnp.where(device >= back[i], m, -BIG)
            top = m if top is None else jnp.maximum(top, m)
        top = top * gain
        total = jnp.zeros((1, rows), f32)
        out = jnp.zeros((width, rows), f32)
        for i in range(5):
            bound = top if i == 2 else jnp.where(device >= back[i], top, BIG)
            e = jnp.exp2(s_ref[i] * gain - bound)
            total += jnp.sum(e, axis=0, keepdims=True)
            eb = e.astype(bf16)
            e_ref[i] = eb
            out += nn(blocks[i][1].T, eb)
        inv = 1.0 / total
        out = out * inv
        grad = qd_ref[h, 1].astype(f32).T
        delta = jnp.sum(grad * out, axis=0, keepdims=True)
        gradn = (grad * inv).astype(bf16)
        gradt = grad.astype(bf16)
        out_ref[h] = out.T
        between(h)
        dq = jnp.zeros((width, rows), f32)
        for i in (4, 3, 0, 1, 2):
            dp = nn(blocks[i][1], gradt)
            eb = e_ref[i]
            ds = (eb.astype(f32) * ((dp - delta) * inv)).astype(bf16)
            grads[i][1] = nt(eb, gradn).astype(bf16)
            grads[i][0] = (nn(ds, query) * scale).astype(bf16)
            dq += nn(blocks[i][0].T, ds)
            if i == 4:
                gthird_copy(h).start()
            if i == 3:
                gpr2_copy(h).start()
                ahead(h)
            if i == 0:
                settle_far(h)
            if i == 1:
                settle_near(h)
        dq_ref[h] = (dq * scale).T

    def settle_far(h):
        gthird_copy(h).got()
        t = bthird_ref[h].astype(f32)
        gfar_ref[h] = (gfar_ref[h].astype(f32) + jnp.where(odd, t, 0.0)).astype(bf16)
        bfar_copy(h).start()

    def settle_near(h):
        gpr2_copy(h).got()
        gr2_ref[h] = (gr2_ref[h].astype(f32) + jnp.where(two_in, bpr2_ref[h].astype(f32), 0.0)).astype(bf16)
        if square:
            relayed(h, gdiag_copy(h).start)
        br2_copy(h).start()

    def ahead(h):
        @pl.when(h < 2)
        def _():
            advance(h + 1)

        if square:
            @pl.when((h == 1) & one)
            def _():
                for i in range(2):
                    cross_copy(2, i).copy.start()

    def late(h, now):
        if square:
            @pl.when(now & zero)
            def _():
                gdiag_copy(h).copy.wait_recv()
                gpass_copy(h).copy.start()

    def between(h):
        if square:
            @pl.when(h == 0)
            def _():
                scan_middle(0)
                for g in range(2, heads):
                    outward(g)

            @pl.when(h == middle_at)
            def _():
                scan_middle(1)

    advance(0)
    prefix_at, middle_at = (PREFIX_AT - chip // 2, last - 2 * (chip // 2) + chip // 3) if square else (PREFIX_AT, last)

    @pl.loop(0, heads)
    def _(h):
        @pl.when(h == prefix_at)
        def _():
            scan_end(0)
            linear_forward()
            pair_copy(1).start()
            scan_begin(1)

        @pl.when(h == 2)
        def _():
            crosses(3, Copy.start)
            advance(3)

        late(0, h == 2)
        window(h)

    linear_backward_queries()
    late(1, True)
    scan_end(1)
    linear_backward_keys()
    for d in range(1, count):
        rs_copy(d).start()
    linear_outputs()
    for d in range(1, count):
        rs_copy(d).got()
    part = map_ref[pl.ds(device * chunk, chunk)]
    for d in range(1, count):
        part += rs_ref[d - 1]
    fin_ref[0] = part
    for d in range(1, lanes):
        hx_copy(d).start()
    turn(lambda r: raw_ref.at[0, r], lambda r: (out_ref[:, r] + lin_ref[:, r]).astype(bf16))
    stores[0].start()
    turn(lambda r: raw_ref.at[1, r], lambda r: dq_ref[:, r].astype(bf16))
    stores[1].start()

    @pl.loop(0, heads)
    def _(h):
        kvl_ref[h] += gown_ref[h].astype(f32) + jnp.where(even, bthird_ref[h].astype(f32), 0.0)

    part = None
    for d in range(1, lanes):
        came = lax.rem(lane + lanes - d, lanes)
        Copy(fin_ref.at[0], hx_ref.at[came], hx_send.at[d - 1], hx_recv.at[d - 1], {"head": lax.rem(lane + d, lanes)}).got()
    hx_ref[lane] = fin_ref[0]
    part = hx_ref[0]
    for d in range(1, lanes):
        part += hx_ref[d]
    fin_ref[1] = part
    for d in range(1, count):
        ag_copy(d).start()
    gmap_ref[pl.ds(device * chunk, chunk)] = part

    @pl.loop(0, heads)
    def _(h):
        br2_copy(h).got()
        bfar_copy(h).got()
        if square:
            relayed(h, gpass_copy(h).got)

    for i in range(2):
        turn(lambda r: raw_ref.at[2 + i, r], lambda r: (kvl_ref[:, i, r] + br2_ref[:, i, r].astype(f32) + bfar_ref[:, i, r].astype(f32)).astype(bf16))
        stores[2 + i].start()

    for d in range(1, count):
        came = lax.rem(device + count - d, count)
        Copy(fin_ref.at[1], gmap_ref.at[pl.ds(came * chunk, chunk)], ag_send.at[d - 1], ag_recv.at[d - 1], {"seq": lax.rem(device + d, count)}).got()
    for i in range(gmap_ref.shape[0] // width):
        gmap_out[:, i * width : (i + 1) * width] = gmap_ref[pl.ds(i * width, width)]
    for store in stores:
        store.wait()
    for d in range(1, count):
        rs_copy(d).sent()
        ag_copy(d).sent()
    for d in range(1, lanes):
        hx_copy(d).sent()
    for p in range(2):
        pair_copy(p).sent()
        total_copy(p).sent()
        if square:
            side_copy(p).sent()
            over_copy(p).sent()
        else:
            for d in chips:
                slot_copy(p, d).sent()

    @pl.loop(0, heads)
    def _(h):
        for copy in (far_copy, r2_copy, pr2_copy, own_copy, relay_copy, gthird_copy, gpr2_copy, br2_copy, bfar_copy):
            copy(h).sent()
        crosses(h, Copy.sent)
        diagonals(h, Copy.sent)
        if square:
            relayed(h, gdiag_copy(h).sent)
            relayed(h, gpass_copy(h).sent)


def on_device(count, lanes, queries, key_vectors, value_vectors, feature_map, cotangent):
    rows, heads, width = queries.shape
    feats = feature_map.shape[1]
    sds = jax.ShapeDtypeStruct
    vmem = pl.BlockSpec(memory_space=pltpu.VMEM)
    hbm = pl.BlockSpec(memory_space=pl.ANY)
    V = pltpu.VMEM
    sem = pltpu.SemaphoreType.DMA
    flat = feats
    chunk = flat // count
    two = V((heads, 2, rows, width), bf16)
    wide = V((heads, rows, width), f32)
    state = V((2, heads, feats, width), f32)
    part = V((2, heads // 2, feats, width), f32)
    chips = count // 2 - 1
    low = sds((rows, heads, width), bf16)
    results = pl.pallas_call(
        functools.partial(kernel, count, lanes),
        out_shape=(low, low, low, low, sds((width, feats), f32)),
        in_specs=[hbm, hbm, hbm, vmem, hbm],
        out_specs=(hbm, hbm, hbm, hbm, vmem),
        scratch_shapes=[V((4, rows, heads, width), bf16), sem((2, 4)), two, two, wide, V((flat, width), f32)] + [two] * 14 + [
            V((5, rows, rows), f32), V((5, rows, rows), bf16),
            V((heads, rows, feats), f32), V((heads, rows, feats), f32), V((heads, rows, rows), bf16),
            wide, V((heads, rows, width), bf16), wide, V((heads, 2, rows, width), f32),
            state, state, V((2, heads // 2, feats, width), bf16), V((2, chips, heads // 2, feats, width), bf16), part, part, state,
            V((flat, width), f32), V((count - 1, chunk, width), f32), V((lanes, chunk, width), f32), V((2, chunk, width), f32),
            sem((9, heads)), sem((9, heads)), sem((6, heads)), sem((6, heads)), sem((2, 2)), sem((2, 2)),
            sem((2, chips)), sem((2, chips)), sem((count - 1,)), sem((count - 1,)), sem((lanes - 1,)), sem((lanes - 1,)),
            sem((count - 1,)), sem((count - 1,)),
        ],
        compiler_params=pltpu.CompilerParams(vmem_limit_bytes=60 * 2**20, collective_id=0, has_side_effects=True),
        name="attention",
    )(queries, key_vectors, value_vectors, feature_map, cotangent)
    return hand_over(results)


def hand_over_kernel(*refs):
    number = len(refs) // 3
    came, gives, held, sems = refs[:number], refs[number : 2 * number], refs[2 * number : 3 * number], refs[-1]
    loads = [pltpu.make_async_copy(came[i], held[i], sems.at[0, i]) for i in range(number)]
    stores = [pltpu.make_async_copy(held[i], gives[i], sems.at[1, i]) for i in range(number)]
    for load in loads:
        load.start()
    for load, store in zip(loads, stores):
        load.wait()
        store.start()
    for store in stores:
        store.wait()


def hand_over(results):
    anywhere = pl.BlockSpec(memory_space=pl.ANY)
    return pl.pallas_call(
        hand_over_kernel,
        out_shape=tuple(jax.ShapeDtypeStruct(x.shape, x.dtype) for x in results),
        in_specs=[anywhere] * len(results),
        out_specs=(anywhere,) * len(results),
        scratch_shapes=[pltpu.VMEM(x.shape, x.dtype) for x in results] + [pltpu.SemaphoreType.DMA((2, len(results)))],
        name="hand_over",
    )(*results)


def solution(mesh):
    spread = P("seq", "head", None)
    return jax.shard_map(
        functools.partial(on_device, mesh.shape["seq"], mesh.shape["head"]),
        mesh=mesh,
        in_specs=(spread, spread, spread, P(), spread),
        out_specs=(spread, spread, spread, spread, P()),
        check_vma=False,
    )
```
